32 devices in a mesh: groups: 2 (over x), expert: 16 (over z, y, core).
Axes of the slice: x: 2, y: 2, z: 4, core: 2. Of those that a mesh axis runs over, the one named last changes fastest.
Arguments:
- residual: bfloat16 [512, 2880], P(('groups', 'expert')), parts along dimension 0, may hold values from -6 to 6
- norm_gain: float32 [2880], replicated, may hold values from 0.1 to 1.9
- expert_ids: int32 [512, 4], P(('groups', 'expert')), parts along dimension 0, may hold values from 0 to 7, all different within a row; in each aligned block of 16 rows (0 to 15, 16 to 31, ...) at most 16 rows name the same one
- expert_weights: float32 [512, 4], P(('groups', 'expert')), parts along dimension 0, may hold values from 0.2 to 1
- gate_proj: bfloat16 [16, 2880, 720], P('expert'), may hold values from -0.109375 to 0.109375
- up_proj: bfloat16 [16, 2880, 720], P('expert'), may hold values from -0.109375 to 0.109375
- down_proj: bfloat16 [16, 720, 2880], P('expert'), may hold values from -0.15625 to 0.15625
Outputs:
- mixed: bfloat16 [512, 2880], P(('groups', 'expert')), parts along dimension 0
The draws below stay inside these ranges and needn't reach their ends.
There are 2 independent parts, one for each index of `groups`. The reference program is written for one: setup_inputs(seed, part) draws one part's arguments, and reference() takes and returns one part's arrays. A program takes and returns all parts, laid end to end along the dimension named above; an argument that names none is the same for every part. Nothing has to cross between parts.
Inputs may be any that keep to these rules, and one draw needn't show every extreme that they name: `expert_ids`: in each aligned block of 16 rows (the rows of one device) no expert is named by more than 16 entries.
All inputs are finite; a program needn't handle non-finite values.
Results may differ from the reference program's by a relative error of at most 0.0063.
Values may be sent and summed in bfloat16 or wider, within the bound.
A program may use at most 64 MiB of HBM per device.

```python
import math
import jax
import jax.numpy as jnp
import numpy as np
from jax import lax

D = 2880
FF = 1440
HALF = 720
TOP = 4
EXPERTS = 8
REQ_DEV = 16
CAP = 16
TOKENS = 256
N_EXPERT = 16


def block_levels(key, dims, pieces, low, largest):
    def one(position, blocks):
        steps = jax.random.uniform(jax.random.fold_in(jax.random.fold_in(key, 6), position), (blocks,), jnp.float32, low / len(pieces), largest / len(pieces))
        return jnp.repeat(jnp.exp(steps), dims[position] // blocks).reshape((-1,) + (1,) * (len(dims) - position - 1))

    factor_of = one(*pieces[0])
    for cut in pieces[1:]:
        factor_of = factor_of * one(*cut)
    return factor_of


def deal_out(own_key, own, number, rows, count, top, bound, lean):
    sequence = jax.random.permutation(own_key, count)
    packed, usual = portions_of(count, rows * top, bound, lean, True), portions_of(count, rows * top, bound, lean, False)
    places = jnp.arange(count)

    def named(sizes, rotation):
        used = int((sizes > 0).sum())
        fixed = max(1, used // 4)
        shifted = fixed + (places - fixed + rotation * (used - fixed)) % max(1, count - fixed)
        return jnp.zeros((count,), jnp.int32).at[sequence[jnp.where(places < fixed, places, shifted)]].set(jnp.asarray(sizes, jnp.int32))

    sizes = jnp.where(number % 4 == 0, named(packed, number // 4), named(usual, number - number // 4 - 1))
    mixed = jax.random.permutation(jax.random.fold_in(own, 3), count)
    donor, taker = mixed[0:count // 2 * 2:2], mixed[1:count // 2 * 2:2]
    room = jnp.minimum(sizes[donor] - 1, bound - sizes[taker]) // 2
    room = jnp.where((donor == sequence[0]) | (taker == sequence[0]) | (sizes[taker] == 0), 0, jnp.maximum(room, 0))
    shifted = jax.random.randint(jax.random.fold_in(own, 4), (count // 2,), 0, 1 << 20) % (room + 1)
    sizes = sizes.at[donor].add(-shifted).at[taker].add(shifted)
    items = jnp.searchsorted(jnp.cumsum(sizes), jnp.arange(rows * top), side="right").astype(jnp.int32)
    grid = items.reshape(top, rows).T
    grid = grid[jax.random.permutation(jax.random.fold_in(own, 1), rows)]
    rotation = jax.random.randint(jax.random.fold_in(own, 2), (rows, 1), 0, top)
    return jnp.take_along_axis(grid, (jnp.arange(top)[None, :] + rotation) % top, axis=1)


def portions_of(amount, total, most, lean, full):
    loads = [(1 << 20) // math.isqrt(grade ** lean) + 1 for grade in range(1, amount + 1)]
    largest = most if full else min(most, max(-(-total // amount), total * loads[0] // sum(loads)))
    least = 1 if total - largest >= amount - 1 else 0
    counts, rest = [largest] + [least] * (amount - 1), total - largest - least * (amount - 1)
    while rest > 0:
        candidates = [i for i in range(1, amount) if counts[i] < largest] or [i for i in range(1, amount) if counts[i] < most]
        pool, left = sum([loads[i] for i in candidates]), rest
        for i in candidates:
            addition = min(most - counts[i], max(1, left * loads[i] // pool), rest)
            counts[i] = counts[i] + addition
            rest = rest - addition
    return np.array(counts)


def normal_values(stream_key, shape, scale, bound, shards=(), dtype=jnp.bfloat16):
    factor_of = block_levels(stream_key, shape, shards, -0.22, 0.18) if shards else 1.0
    array = jax.random.normal(stream_key, shape, jnp.float32) * scale * factor_of
    return jnp.minimum(jnp.maximum(array, -bound), bound).astype(dtype)


def setup_inputs(seed: int = 0, part: int = 0) -> dict:
    streams_of = jax.random.split(jax.random.key(seed), 8)
    own_keys = jax.random.split(jax.random.fold_in(streams_of[7], part), 8)
    residual = normal_values(own_keys[0], (TOKENS, D), 1.0, 6.0, ((0, 16),))
    norm_gain = jnp.clip(1.0 + 0.18 * jax.random.normal(streams_of[1], (D,), jnp.float32), 0.1, 1.9)
    expert_ids_keys = jax.random.split(jax.random.fold_in(own_keys[2], 1), TOKENS // REQ_DEV)
    expert_ids_turns = jax.random.permutation(jax.random.fold_in(own_keys[2], 3), TOKENS // REQ_DEV)
    expert_ids = jax.vmap(lambda own, number: deal_out(jax.random.fold_in(own_keys[2], 2), own, number, REQ_DEV, EXPERTS, TOP, CAP, 2))(expert_ids_keys, expert_ids_turns).reshape((TOKENS, TOP))
    expert_weights = jnp.clip(0.2 + 0.8 * jax.random.uniform(own_keys[3], (TOKENS, TOP), jnp.float32) ** block_levels(own_keys[3], (TOKENS, TOP), ((0, 16),), -0.2, 0.2), 0.2, 1.0)
    gate_proj = normal_values(streams_of[4], (2 * EXPERTS, D, HALF), D ** -0.5, 0.109375, ((0, 16),))
    up_proj = normal_values(streams_of[5], (2 * EXPERTS, D, HALF), D ** -0.5, 0.109375, ((0, 16),))
    down_proj = normal_values(streams_of[6], (2 * EXPERTS, HALF, D), FF ** -0.5, 0.15625, ((0, 16),))
    return {"residual": residual, "norm_gain": norm_gain, "expert_ids": expert_ids, "expert_weights": expert_weights, "gate_proj": gate_proj, "up_proj": up_proj, "down_proj": down_proj}


def expert_half(flat, gate_w, up_w, down_w):
    gate = jnp.dot(flat, gate_w, preferred_element_type=jnp.float32)
    upper = jnp.dot(flat, up_w, preferred_element_type=jnp.float32)
    act = (gate * jax.nn.sigmoid(1.702 * gate) * (upper + 1.0)).astype(jnp.bfloat16)
    return jnp.dot(act, down_w, preferred_element_type=jnp.float32).astype(jnp.bfloat16)

def reference(residual, norm_gain, expert_ids, expert_weights, gate_proj, up_proj, down_proj):
    devices = N_EXPERT
    experts = devices // 2
    width = REQ_DEV * TOP
    x = residual.astype(jnp.float32)
    scale = lax.rsqrt(lax.optimization_barrier(jnp.mean(x * x, axis=-1, keepdims=True)) + 1e-05)
    normed = (x * scale * norm_gain.astype(jnp.float32)).astype(jnp.bfloat16)
    flat = expert_ids.reshape(devices, width).astype(jnp.int32)
    onehot = (flat[:, :, None] == jnp.arange(experts).astype(jnp.int32)[None, None, :]).astype(jnp.int32)
    slot = (lax.optimization_barrier(jnp.sum(onehot * jnp.cumsum(onehot, axis=1), axis=-1)) - 1).astype(jnp.int32)
    source = jnp.broadcast_to(jnp.arange(devices).astype(jnp.int32)[:, None], (devices, width))
    token = (jnp.arange(width).astype(jnp.int32) // TOP)[None, :] + source * REQ_DEV
    buffer = jnp.zeros((experts, devices, CAP, D), jnp.bfloat16).at[flat, source, slot].set(normed[token])

    def run(items):
        block, gate_w, up_w, down_w = items
        first = expert_half(block, gate_w[0], up_w[0], down_w[0])
        second = expert_half(block, gate_w[1], up_w[1], down_w[1])
        return (first.astype(jnp.float32) + second.astype(jnp.float32)).astype(jnp.bfloat16)
    outs = lax.map(run, (buffer.reshape(experts, devices * CAP, D), gate_proj.reshape(experts, 2, D, HALF), up_proj.reshape(experts, 2, D, HALF), down_proj.reshape(experts, 2, HALF, D)))
    outs = outs.reshape(experts, devices, CAP, D)
    picked = outs[flat, source, slot].reshape(devices, REQ_DEV, TOP, D).astype(jnp.float32)
    weights = expert_weights.reshape(devices, REQ_DEV, TOP, 1)
    mixed = x.reshape(devices, REQ_DEV, D) + lax.optimization_barrier(jnp.sum(weights * picked, axis=2))
    return mixed.reshape(TOKENS, D).astype(jnp.bfloat16)
```

```python
import functools

import jax
import jax.numpy as jnp
from jax import lax
from jax.experimental import pallas as pl
from jax.experimental.pallas import tpu as pltpu
from jax.sharding import PartitionSpec as P

BF16 = jnp.bfloat16
F32 = jnp.float32
LANES = 128


def partner(value, axis, bit):
    mask = 2**bit
    pairs = [(source, source ^ mask) for source in range(lax.axis_size(axis))]
    return lax.ppermute(value, axis, pairs)


def expert_half(block, gate_w, up_w, down_w):
    flat = block.reshape(-1, block.shape[-1])
    gate = jnp.dot(flat, gate_w, preferred_element_type=jnp.float32)
    upper = jnp.dot(flat, up_w, preferred_element_type=jnp.float32)
    act = (gate * jax.nn.sigmoid(1.702 * gate) * (upper + 1.0)).astype(jnp.bfloat16)
    out = jnp.dot(act, down_w, preferred_element_type=jnp.float32).astype(jnp.bfloat16)
    return out.reshape(block.shape[:-1] + (down_w.shape[1],))


def slotted(residual, norm_gain, expert_ids, expert_weights, gate_proj, up_proj, down_proj):
    rows, model = residual.shape
    chosen = expert_ids.shape[1]
    devices = lax.axis_size("expert")
    experts = devices // 2
    capacity = 2 * rows * chosen // experts
    half_cap = capacity // 2
    gate_w, up_w, down_w = (gate_proj[0], up_proj[0], down_proj[0])
    x = residual.astype(jnp.float32)
    scale = lax.rsqrt(jnp.mean(x * x, axis=-1, keepdims=True) + 1e-05)
    normed = (x * scale * norm_gain).astype(jnp.bfloat16)
    flat_ids = expert_ids.reshape(rows * chosen)
    onehot = (
        flat_ids[:, None] == lax.broadcasted_iota(jnp.int32, (rows * chosen, experts), 1)
    ).astype(jnp.int32)
    slot = jnp.sum(onehot * jnp.cumsum(onehot, axis=0), axis=1) - 1
    position = flat_ids * capacity + slot
    pick = (
        position[:, None] == lax.broadcasted_iota(jnp.int32, (rows * chosen, experts * capacity), 1)
    ).astype(jnp.float32)
    place_rows = jnp.sum(pick.reshape(rows, chosen, experts * capacity), axis=1)
    send = lax.dot_general(
        place_rows.astype(jnp.bfloat16),
        normed,
        (((0,), (0,)), ((), ())),
        preferred_element_type=jnp.float32,
    )
    send = send.astype(jnp.bfloat16).reshape(experts, capacity, model)
    outgoing = send.reshape(experts, 2, half_cap, model).reshape(devices, half_cap, model)
    arrived = lax.all_to_all(outgoing, "expert", split_axis=0, concat_axis=0, tiled=True)
    other = partner(arrived, "expert", 0)
    both = expert_half(jnp.stack((arrived, other)), gate_w, up_w, down_w)
    returned = partner(both[1], "expert", 0)
    finished = (both[0].astype(jnp.float32) + returned.astype(jnp.float32)).astype(jnp.bfloat16)
    back = lax.all_to_all(finished, "expert", split_axis=0, concat_axis=0, tiled=True)
    results = back.reshape(experts, capacity, model)
    weighted = jnp.sum(
        (pick * expert_weights.reshape(rows * chosen)[:, None]).reshape(
            rows, chosen, experts * capacity
        ),
        axis=1,
    )
    combined = jnp.dot(
        weighted,
        results.reshape(experts * capacity, model).astype(jnp.float32),
        precision=lax.Precision.HIGHEST,
    )
    return (x + combined).astype(jnp.bfloat16)


def cuts(total, shares):
    unit = 2 * LANES
    whole = sum(shares)
    ends = [round(total * sum(shares[: n + 1]) / whole / unit) * unit for n in range(len(shares))]
    ends = sorted(set(min(max(e, unit), total) for e in ends[:-1]) | {total})
    starts = [0] + ends[:-1]
    return [(s, e - s) for s, e in zip(starts, ends) if e > s]


def kernel(
    experts, in_cuts, out_cuts,
    res_ref, gain_ref, ids_ref, wts_ref, gate_hbm, up_hbm, down_hbm, out_ref,
    gate_v, up_v, down_v, xg, gacc, uacc, act_v, part, core_r, y_s, y_r, z_s, z_r,
    w_sem, d_sem, agl_s, agr_s, agz_r, agy_s, agy_r, agc_s, agc_r,
    rc_s, rc_r, ry_s, ry_r, rz_s, rz_r,
):
    line = 4
    last = line - 1
    rows, model = res_ref.shape
    extra = xg.shape[1] - model
    tokens = 4 * line * rows
    half, pair = tokens // 2, tokens // 4
    me = lax.axis_index("expert")
    core = lax.rem(me, 2)
    y = lax.rem(me // 2, 2)
    z = me // 4
    side, low = z // 2, lax.rem(z, 2)
    near, far = z + 1 - 2 * low, lax.rem(z + 2, line)

    def device(z_, y_, c_):
        return (z_ * 2 + y_) * 2 + c_

    def row(z_, y_, c_):
        at = (((z_ // 2 * 2 + c_) * 2 + lax.rem(z_, 2)) * 2 + y_) * rows
        return pl.multiple_of(at, rows)

    def remote(src, dst, send, recv, target):
        return pltpu.make_async_remote_copy(
            src_ref=src, dst_ref=dst, send_sem=send, recv_sem=recv,
            device_id={"expert": target}, device_id_type=pl.DeviceIdType.MESH,
        )

    y_dev = device(z, 1 - y, core)
    c_dev = device(z, y, 1 - core)
    n_dev = device(near, y, core)
    f_dev = device(far, y, core)

    barrier = pltpu.get_barrier_semaphore()
    inner = jnp.logical_and(z > 0, z < last)

    def greet(peer):
        pl.semaphore_signal(
            barrier, inc=1, device_id={"expert": peer}, device_id_type=pl.DeviceIdType.MESH
        )

    greet(y_dev)
    greet(c_dev)
    greet(n_dev)
    greet(f_dev)
    pl.when(inner)(lambda: greet(device(last - z, y, core)))

    loads = []
    for n, (hbm, vmem) in enumerate(((gate_hbm, gate_v), (up_hbm, up_v))):
        loads.append(pltpu.make_async_copy(hbm.at[0], vmem, w_sem.at[n]))
    loads.append(pltpu.make_async_copy(down_hbm.at[0], down_v, d_sem))
    for copy in loads:
        copy.start()

    x = res_ref[...].astype(F32)
    scale = lax.rsqrt(jnp.mean(x * x, axis=-1, keepdims=True) + 1e-05)
    normed = (x * scale * gain_ref[...]).astype(BF16)
    named = lax.broadcasted_iota(jnp.int32, (extra, rows), 0)
    high = jnp.zeros((extra, rows), F32)
    under = jnp.zeros((extra, rows), F32)
    for k in range(ids_ref.shape[0]):
        ids = ids_ref[k : k + 1, :]
        high = high + jnp.where(ids == named, wts_ref[k : k + 1, :], 0.0)
        under = under + jnp.where(ids + experts == named, wts_ref[k : k + 1, :], 0.0)
    rest = under - under.astype(BF16).astype(F32)
    shares = jnp.transpose(high + rest).astype(BF16)
    mine = pl.ds(row(z, y, core), rows)
    xg[mine, 0:model] = normed
    xg[mine, model : model + extra] = shares

    pl.semaphore_wait(barrier, 4 + jnp.where(inner, 1, 0))

    chunks = len(in_cuts)

    def columns(k):
        at, wide = in_cuts[k]
        return pl.ds(at, wide + extra if k == chunks - 1 else wide)

    def block(k, z_, y_, c_):
        return xg.at[pl.ds(row(z_, y_, c_), rows), columns(k)]

    def pass_left(k, z_):
        at = block(k, z_, y, core)
        return remote(at, at, agl_s.at[k, z_], agz_r.at[k, z_], device(z - 1, y, core))

    def pass_right(k, z_):
        at = block(k, z_, y, core)
        return remote(at, at, agr_s.at[k, z_], agz_r.at[k, z_], device(z + 1, y, core))

    def pass_y(k, z_):
        at = block(k, z_, y, core)
        return remote(at, at, agy_s.at[k], agy_r.at[k, z_], y_dev)

    def from_y(k, z_):
        at = block(k, z_, 1 - y, core)
        return remote(at, at, agy_s.at[k], agy_r.at[k, z_], y_dev)

    def pass_core(k, z_, y_):
        at = block(k, z_, y_, core)
        remote(at, at, agc_s.at[k], agc_r.at[k], c_dev).start()

    def bulk(k, count):
        return xg.at[pl.ds(0, count * rows), columns(k)]

    def from_right(k, d):
        pass_left(k, z + d).wait_recv()
        pass_y(k, z + d).start()
        pl.when(z > 0)(lambda: pass_left(k, z + d).start())
        pass_core(k, z + d, y)

    def from_left(k, d):
        pass_right(k, z - d).wait_recv()
        pass_y(k, z - d).start()
        pl.when(z < last)(lambda: pass_right(k, z - d).start())
        pass_core(k, z - d, y)

    def line_step(k, d):
        pl.when(z + d <= last)(lambda: from_right(k, d))
        pl.when(z - d >= 0)(lambda: from_left(k, d))

    for k in range(chunks):
        pass_y(k, z).start()
        pl.when(z > 0)(lambda: pass_left(k, z).start())
        pl.when(z < last)(lambda: pass_right(k, z).start())
    for k in range(chunks):
        pass_core(k, z, y)
    for d in range(1, line):
        for k in range(chunks):
            line_step(k, d)
    for k in range(chunks):
        for there in range(line):
            from_y(k, there).wait_recv()
            pass_core(k, there, 1 - y)

    def arrive(k):
        at = bulk(k, 2 * line)
        remote(at, at, agc_s.at[k], agc_r.at[k], c_dev).wait_recv()

    def drain_gather():
        for k in range(chunks):
            at = bulk(k, line)
            remote(at, at, agy_s.at[k], agy_r.at[k, 0], y_dev).wait_send()
            at = bulk(k, 2 * line)
            remote(at, at, agc_s.at[k], agc_r.at[k], c_dev).wait_send()
            for z_ in range(line):
                pl.when(jnp.logical_and(z > 0, z <= z_))(
                    lambda: pass_left(k, z_).wait_send()
                )
                pl.when(jnp.logical_and(z < last, z >= z_))(
                    lambda: pass_right(k, z_).wait_send()
                )

    expert = me // 2
    swap = (((1,), (1,)), ((), ()))

    loads[0].wait()
    loads[1].wait()
    for k in range(chunks - 1):
        arrive(k)
    split = in_cuts[-1][0]
    for vmem, acc in ((gate_v, gacc), (up_v, uacc)):
        acc[...] = lax.dot_general(
            vmem[:, 0:split], xg[:, 0:split], swap, preferred_element_type=F32
        )
    arrive(chunks - 1)
    loads[2].wait()
    gate, upper = (
        acc[...] + lax.dot_general(
            vmem[:, split:model], xg[:, split:model], swap, preferred_element_type=F32
        )
        for vmem, acc in ((gate_v, gacc), (up_v, uacc))
    )
    act_v[...] = (gate * jax.nn.sigmoid(1.702 * gate) * (upper + 1.0)).astype(BF16).T

    bases = (
        pl.multiple_of((1 - side) * half, half),
        pl.multiple_of(side * half, half),
    )
    lanes = lax.broadcasted_iota(jnp.int32, (tokens, extra), 1)
    ours = jnp.logical_or(lanes == expert, lanes == expert + experts)
    weight = jnp.sum(
        jnp.where(ours, xg[:, model : model + extra].astype(F32), 0.0), axis=1, keepdims=True
    )
    outs = range(len(out_cuts))

    def core_copy(h, j):
        at, wide = out_cuts[j]
        cols = pl.ds(at, wide)
        theirs = pl.multiple_of(bases[h] + (1 - core) * pair, pair)
        return remote(
            part.at[pl.ds(theirs, pair), cols],
            core_r.at[pl.ds(h * pair, pair), cols],
            rc_s, rc_r.at[h, j], c_dev,
        )

    def product(j):
        at, wide = out_cuts[j]
        value = jnp.dot(act_v[...], down_v[:, at : at + wide], preferred_element_type=F32)
        part[:, at : at + wide] = (value * weight).astype(BF16)
        core_copy(0, j).start()

    def pair_sum(h, j, low_, y_):
        at, wide = out_cuts[j]
        inside = (low_ * 2 + y_) * rows
        theirs = core_r[pl.ds(pl.multiple_of(h * pair + inside, rows), rows), at : at + wide]
        spot = pl.multiple_of(bases[h] + core * pair + inside, rows)
        here = part[pl.ds(spot, rows), at : at + wide]
        return theirs.astype(F32) + here.astype(F32)

    spots = ((0, 2), (2, 1), (3, 1))
    FAR, NEAR, OWN = range(3)

    def y_copy(g, j):
        at, wide = out_cuts[j]
        first, count = spots[g]
        spot = (pl.ds(first * rows, count * rows), pl.ds(at, wide))
        return remote(y_s.at[spot], y_r.at[spot], ry_s, ry_r.at[g, j], y_dev)

    def slot(i, j):
        at, wide = out_cuts[j]
        return slice(i * rows, (i + 1) * rows), slice(at, at + wide)

    def y_send(g, j):
        if g == FAR:
            core_copy(0, j).wait_recv()
            y_s[slot(0, j)] = pair_sum(0, j, low, 1 - y).astype(BF16)
            y_s[slot(1, j)] = pair_sum(0, j, 1 - low, 1 - y).astype(BF16)
        elif g == NEAR:
            core_copy(1, j).wait_recv()
            y_s[slot(2, j)] = pair_sum(1, j, 1 - low, 1 - y).astype(BF16)
        else:
            y_s[slot(3, j)] = pair_sum(1, j, low, 1 - y).astype(BF16)
        y_copy(g, j).start()

    def z_copy(i, j):
        at, wide = out_cuts[j]
        spot = (pl.ds(i * rows, rows), pl.ds(at, wide))
        return remote(
            z_s.at[spot], z_r.at[spot], rz_s, rz_r.at[i, j],
            f_dev if i == 1 else n_dev,
        )

    def cross(j):
        y_copy(FAR, j).wait_recv()
        total = pair_sum(0, j, 1 - low, y) + y_r[slot(1, j)].astype(F32)
        z_s[slot(0, j)] = total.astype(BF16)
        z_copy(0, j).start()

    def leap(j):
        z_copy(0, j).wait_recv()
        total = pair_sum(0, j, low, y) + y_r[slot(0, j)].astype(F32)
        total = total + z_r[slot(0, j)].astype(F32)
        z_s[slot(1, j)] = total.astype(BF16)
        z_copy(1, j).start()

    def beside(j):
        y_copy(NEAR, j).wait_recv()
        total = pair_sum(1, j, 1 - low, y) + y_r[slot(2, j)].astype(F32)
        z_s[slot(2, j)] = total.astype(BF16)
        z_copy(2, j).start()

    def finish(j):
        at, wide = out_cuts[j]
        y_copy(OWN, j).wait_recv()
        z_copy(2, j).wait_recv()
        z_copy(1, j).wait_recv()
        total = pair_sum(1, j, low, y) + y_r[slot(3, j)].astype(F32)
        total = total + z_r[slot(2, j)].astype(F32) + z_r[slot(1, j)].astype(F32)
        out_ref[:, at : at + wide] = (
            res_ref[:, at : at + wide].astype(F32) + total
        ).astype(BF16)

    count = len(out_cuts)
    lag = 2
    for n in range(count + lag):
        if n < count:
            product(n)
        if n == count - 1:
            for j in outs:
                core_copy(1, j).start()
        if n >= lag:
            y_send(FAR, n - lag)
    for group in (NEAR, OWN):
        for j in outs:
            y_send(group, j)
    plan = sorted(
        [(j + 0.0, 0, j) for j in outs]
        + [(j + 2.1, 1, j) for j in outs]
        + [(j / 2 + 3.4, 2, j) for j in outs]
    )
    for _, stage, j in plan:
        (cross, leap, beside)[stage](j)
    for j in outs:
        finish(j)
    drain_gather()
    remote(part.at[pl.ds(0, half)], core_r, rc_s, rc_r.at[0, 0], c_dev).wait_send()
    remote(y_s, y_r, ry_s, ry_r.at[0, 0], y_dev).wait_send()
    remote(z_s, z_r, rz_s, rz_r.at[0, 0], n_dev).wait_send()


def fused(residual, norm_gain, expert_ids, expert_weights, gate_proj, up_proj, down_proj):
    rows, model = residual.shape
    hidden = gate_proj.shape[2]
    devices = lax.axis_size("expert")
    experts = devices // 2
    line = devices // 4
    in_cuts = cuts(model, (3, 3, 3, 2))
    ins = len(in_cuts)
    tokens = rows * devices
    width = -(-(model + 2 * experts) // LANES) * LANES
    out_cuts = cuts(model, (2, 3, 3, 3))
    outs = len(out_cuts)
    vmem = pl.BlockSpec(memory_space=pltpu.VMEM)
    hbm = pl.BlockSpec(memory_space=pl.ANY)
    dma = pltpu.SemaphoreType.DMA
    return pl.pallas_call(
        functools.partial(kernel, experts, in_cuts, out_cuts),
        out_shape=pltpu.VMEM((rows, model), BF16),
        in_specs=[vmem] * 4 + [hbm] * 3,
        out_specs=vmem,
        scratch_shapes=[
            pltpu.VMEM((hidden, model), BF16),
            pltpu.VMEM((hidden, model), BF16),
            pltpu.VMEM((hidden, model), BF16),
            pltpu.VMEM((tokens, width), BF16),
            pltpu.VMEM((hidden, tokens), F32),
            pltpu.VMEM((hidden, tokens), F32),
            pltpu.VMEM((tokens, hidden), BF16),
            pltpu.VMEM((tokens, model), BF16),
            pltpu.VMEM((tokens // 2, model), BF16),
            pltpu.VMEM((4 * rows, model), BF16),
            pltpu.VMEM((4 * rows, model), BF16),
            pltpu.VMEM((3 * rows, model), BF16),
            pltpu.VMEM((3 * rows, model), BF16),
            dma((2,)),
            dma,
            dma((ins, line)),
            dma((ins, line)),
            dma((ins, line)),
            dma((ins,)),
            dma((ins, line)),
            dma((ins,)),
            dma((ins,)),
            dma,
            dma((2, outs)),
            dma,
            dma((3, outs)),
            dma,
            dma((3, outs)),
        ],
        compiler_params=pltpu.CompilerParams(
            collective_id=0, has_side_effects=True, vmem_limit_bytes=60 * 1024 * 1024
        ),
    )(
        residual, norm_gain, expert_ids.T, expert_weights.T,
        gate_proj.transpose(0, 2, 1), up_proj.transpose(0, 2, 1), down_proj,
    )


def body(residual, norm_gain, expert_ids, expert_weights, gate_proj, up_proj, down_proj):
    rows = residual.shape[0]
    devices = lax.axis_size("expert")
    capacity = 4 * rows * expert_ids.shape[1] // devices
    dense = capacity >= rows and devices == 16
    form = fused if dense else slotted
    return form(
        residual, norm_gain, expert_ids, expert_weights, gate_proj, up_proj, down_proj
    )


def solution(mesh):
    in_specs = (
        P(("groups", "expert"), None),
        P(),
        P(("groups", "expert"), None),
        P(("groups", "expert"), None),
        P("expert", None, None),
        P("expert", None, None),
        P("expert", None, None),
    )
    out_specs = P(("groups", "expert"), None)
    return jax.shard_map(body, mesh=mesh, in_specs=in_specs, out_specs=out_specs, check_vma=False)
```
